32 devices in a mesh: dp: 4 (over y, x), expert: 8 (over z, core).
Axes of the slice: x: 2, y: 2, z: 4, core: 2. Of those that a mesh axis runs over, the one named last changes fastest.
Arguments:
- inputs: bfloat16 [3, 8, 512, 1024], P(None, 'expert', 'dp'), may hold values from -6 to 6
- w_qkv: bfloat16 [1024, 3072], P(('dp', 'expert')), may hold values from -0.1875 to 0.1875
- w_out: bfloat16 [1024, 1024], P(('dp', 'expert')), may hold values from -0.75 to 0.75
- w_up: bfloat16 [1024, 4096], P(('dp', 'expert')), may hold values from -0.1875 to 0.1875
- w_down: bfloat16 [4096, 1024], P(('dp', 'expert')), may hold values from -0.09375 to 0.09375
- router: bfloat16 [1024, 8], P(('dp', 'expert')), may hold values from -0.125 to 0.125
- mix_weight: bfloat16 [1024, 2], P(('dp', 'expert')), may hold values from -0.125 to 0.125
- norm_gains: float32 [1024, 2], P(('dp', 'expert')), may hold values from 0.5 to 1.5
- norm_biases: float32 [1024, 2], P(('dp', 'expert')), may hold values from -0.6 to 0.6
- expert_input_weights: bfloat16 [8, 1024, 4096], P('expert'), may hold values from -0.1875 to 0.1875
- expert_out: bfloat16 [8, 4096, 1024], P('expert'), may hold values from -0.75 to 0.75
- routes: int32 [3, 8, 512, 1], P(None, 'expert', 'dp'), may hold values from 0 to 7; in each aligned block of 128 rows (0 to 127, 128 to 255, ..., all dimensions but the last counted through in order) at most 48 rows name the same one
- cotangent: bfloat16 [3, 8, 512, 1024], P(None, 'expert', 'dp'), may hold values from -6 to 6
Outputs:
- output: bfloat16 [3, 8, 512, 1024], P(None, 'expert', 'dp')
- d_inputs: float32 [3, 8, 512, 1024], P(None, 'expert', 'dp')
- g_qkv: float32 [1024, 3072], P(('dp', 'expert'))
- g_out: float32 [1024, 1024], P(('dp', 'expert'))
- g_up: float32 [1024, 4096], P(('dp', 'expert'))
- g_down: float32 [4096, 1024], P(('dp', 'expert'))
- g_router: float32 [1024, 8], P(('dp', 'expert'))
- g_mix: float32 [1024, 2], P(('dp', 'expert'))
- g_gains: float32 [1024, 2], P(('dp', 'expert'))
- g_biases: float32 [1024, 2], P(('dp', 'expert'))
- g_expert_in: float32 [8, 1024, 4096], P('expert', None, 'dp')
- g_expert_out: float32 [8, 4096, 1024], P('expert', 'dp')
The draws below stay inside these ranges and needn't reach their ends.
Inputs may be any that keep to these rules, and one draw needn't show every extreme that they name: `routes`: every expert is chosen by some token. Among the 128 tokens of one device in one micro-batch no expert is chosen more than 48 times, and in some such blocks one expert is chosen exactly 48 times.
All inputs are finite; a program needn't handle non-finite values.
Results may differ from the reference program's by a relative error of at most 0.035.
Values may be sent and summed in bfloat16 or wider, within the bound.
No kernel may reach another device: no remote copies, remote signals or barrier semaphores. Data moves between devices by JAX's collectives and lax.ppermute only.
A program may use at most 320 MiB of HBM per device.

```python
import math
import jax
import jax.numpy as jnp
import numpy as np
from jax import lax

D = 1024
HEADS = 16
HEAD_DIM = 64
FF = 4096
EFF = 4096
MICRO = 3
LQ = 128
EXPERTS = 8
SEQS = 8
LEN = 512
CAP = 24
MOST = 48
N_DP = 4


def shard_levels(own_key, extent, pieces, low, largest):
    def one(dim, shards_of):
        draws = jax.random.uniform(jax.random.fold_in(jax.random.fold_in(own_key, 6), dim), (shards_of,), jnp.float32, low / len(pieces), largest / len(pieces))
        return jnp.repeat(jnp.exp(draws), extent[dim] // shards_of).reshape((-1,) + (1,) * (len(extent) - dim - 1))

    factor_of = one(*pieces[0])
    for cut in pieces[1:]:
        factor_of = factor_of * one(*cut)
    return factor_of


def routed_block(key, own, number, rows, number_of, top, reach, slope):
    order = jax.random.permutation(key, number_of)
    crowded, usual = load_shares(number_of, rows * top, reach, slope, True), load_shares(number_of, rows * top, reach, slope, False)
    places = jnp.arange(number_of)

    def named(sizes, offset_by):
        used = int((sizes > 0).sum())
        fixed = max(1, used // 4)
        shifted = fixed + (places - fixed + offset_by * (used - fixed)) % max(1, number_of - fixed)
        return jnp.zeros((number_of,), jnp.int32).at[order[jnp.where(places < fixed, places, shifted)]].set(jnp.asarray(sizes, jnp.int32))

    sizes = jnp.where(number % 4 == 0, named(crowded, number // 4), named(usual, number - number // 4 - 1))
    mixed = jax.random.permutation(jax.random.fold_in(own, 3), number_of)
    giver, taker = mixed[0:number_of // 2 * 2:2], mixed[1:number_of // 2 * 2:2]
    margin = jnp.minimum(sizes[giver] - 1, reach - sizes[taker]) // 2
    margin = jnp.where((giver == order[0]) | (taker == order[0]) | (sizes[taker] == 0), 0, jnp.maximum(margin, 0))
    shifted = jax.random.randint(jax.random.fold_in(own, 4), (number_of // 2,), 0, 1 << 20) % (margin + 1)
    sizes = sizes.at[giver].add(-shifted).at[taker].add(shifted)
    members = jnp.searchsorted(jnp.cumsum(sizes), jnp.arange(rows * top), side="right").astype(jnp.int32)
    grid = members.reshape(top, rows).T
    grid = grid[jax.random.permutation(jax.random.fold_in(own, 1), rows)]
    offset_by = jax.random.randint(jax.random.fold_in(own, 2), (rows, 1), 0, top)
    return jnp.take_along_axis(grid, (jnp.arange(top)[None, :] + offset_by) % top, axis=1)


def load_shares(count, total, limit, lean, full):
    portions = [(1 << 20) // math.isqrt(rank ** lean) + 1 for rank in range(1, count + 1)]
    largest = limit if full else min(limit, max(-(-total // count), total * portions[0] // sum(portions)))
    least = 1 if total - largest >= count - 1 else 0
    counts, surplus = [largest] + [least] * (count - 1), total - largest - least * (count - 1)
    while surplus > 0:
        movable = [i for i in range(1, count) if counts[i] < largest] or [i for i in range(1, count) if counts[i] < limit]
        mass, budget = sum([portions[i] for i in movable]), surplus
        for i in movable:
            addition = min(limit - counts[i], max(1, budget * portions[i] // mass), surplus)
            counts[i] = counts[i] + addition
            surplus = surplus - addition
    return np.array(counts)


def bell_draw(own_key, extent, scale, bound, split=(), kind=jnp.bfloat16):
    values = scale * jax.random.normal(own_key, extent, jnp.float32)
    if split:
        values = values * shard_levels(own_key, extent, split, -0.22, 0.18)
    return jnp.clip(values, -bound, bound).astype(kind)


def setup_inputs(seed: int = 0) -> dict:
    streams_of = jax.random.split(jax.random.key(seed), 14)
    inputs = bell_draw(streams_of[0], (MICRO, SEQS, LEN, D), 1.0, 6.0, ((1, 8), (2, 4)))
    w_qkv = bell_draw(streams_of[1], (D, 3 * D), D ** -0.5, 0.1875, ((0, 32),))
    w_out = bell_draw(streams_of[2], (D, D), (D // 16) ** -0.5, 0.75, ((0, 32),))
    w_up = bell_draw(streams_of[3], (D, FF), D ** -0.5, 0.1875, ((0, 32),))
    w_down = bell_draw(streams_of[4], (FF, D), FF ** -0.5, 0.09375, ((0, 32),))
    router = bell_draw(streams_of[5], (D, EXPERTS), (2 * D) ** -0.5, 0.125, ((0, 32),))
    mix_weight = bell_draw(streams_of[6], (D, 2), (2 * D) ** -0.5, 0.125, ((0, 32),))
    norm_gains = jnp.clip(1.0 + 0.1 * jax.random.normal(streams_of[7], (D, 2), jnp.float32), 0.5, 1.5)
    norm_biases = bell_draw(streams_of[8], (D, 2), 0.1, 0.6, ((0, 32),), jnp.float32)
    expert_input_weights = bell_draw(streams_of[9], (EXPERTS, D, EFF), D ** -0.5, 0.1875, ((0, 8),))
    expert_out = bell_draw(streams_of[10], (EXPERTS, EFF, D), (max(1, EFF // (EXPERTS * EXPERTS))) ** -0.5, 0.75, ((0, 8),))
    routes_keys = jax.random.split(jax.random.fold_in(streams_of[11], 1), MICRO * SEQS * LEN // LQ)
    routes_turns = jax.random.permutation(jax.random.fold_in(streams_of[11], 3), MICRO * SEQS * LEN // LQ)
    routes = jax.vmap(lambda own, number: routed_block(jax.random.fold_in(streams_of[11], 2), own, number, LQ, EXPERTS, 1, MOST, 2))(routes_keys, routes_turns).reshape((MICRO, SEQS, LEN, 1))
    cotangent = bell_draw(streams_of[12], (MICRO, SEQS, LEN, D), 1.0, 6.0, ((1, 8), (2, 4)))
    return {"inputs": inputs, "w_qkv": w_qkv, "w_out": w_out, "w_up": w_up, "w_down": w_down, "router": router, "mix_weight": mix_weight, "norm_gains": norm_gains, "norm_biases": norm_biases, "expert_input_weights": expert_input_weights, "expert_out": expert_out, "routes": routes, "cotangent": cotangent}


@jax.custom_vjp
def low(v):
    return lax.optimization_barrier(v.astype(jnp.bfloat16)).astype(jnp.float32)

@jax.custom_vjp
def low_back(v):
    return v

def low_keep(v):
    return (low(v), None)

def low_pass(kept, grad):
    return (grad,)

def back_keep(v):
    return (v, None)

def back_low(kept, grad):
    return (low(grad),)
low.defvjp(low_keep, low_pass)
low_back.defvjp(back_keep, back_low)
highest = lax.Precision.HIGHEST

def layer_norm(values, gain_vec, bias_vec):
    average = lax.optimization_barrier(jnp.mean(values, axis=-1, keepdims=True))
    centred = values - average
    variance = lax.optimization_barrier(jnp.mean(centred * centred, axis=-1, keepdims=True))
    return centred * lax.rsqrt(variance + 1e-05) * gain_vec + bias_vec

def gelu_tanh(values):
    return jax.nn.gelu(values, approximate=True)

def attention_apply(seq_in, w_qkv, w_out, gain_vec, bias_vec):
    normed = low(layer_norm(seq_in, gain_vec, bias_vec))
    qkv_all = low(low_back(jnp.dot(normed, w_qkv, precision=highest)))
    query = qkv_all[:, :D].reshape(LEN, HEADS, HEAD_DIM)
    key_heads = qkv_all[:, D:2 * D].reshape(LEN, HEADS, HEAD_DIM)
    value_heads = qkv_all[:, 2 * D:].reshape(LEN, HEADS, HEAD_DIM)
    scores = low_back(jnp.einsum('qhd,khd->hqk', query, key_heads, precision=highest) * HEAD_DIM ** (-0.5))
    places = jnp.arange(LEN, dtype=jnp.int32)
    causal = places[:, None] >= places[None, :]
    scores = jnp.where(causal[None], scores, -1e+30)
    attn_probs = low(jax.nn.softmax(scores, axis=-1))
    mixed_heads = low(low_back(jnp.einsum('hqk,khd->qhd', attn_probs, value_heads, precision=highest)))
    mixed_heads = mixed_heads.reshape(LEN, D)
    return seq_in + low_back(jnp.dot(mixed_heads, w_out, precision=highest))

def feedforward_block(residual, route_mb, w_up, w_down, router, mix_weight, gain_vec, bias_vec, expert_input_weights, expert_out):
    normed = layer_norm(residual, gain_vec, bias_vec)
    normed_low = low(normed)
    up_dense = low_back(jnp.einsum('sti,if->stf', normed_low, w_up, precision=highest))
    act_dense = low(gelu_tanh(up_dense))
    dense_out = low_back(jnp.einsum('stf,fi->sti', act_dense, w_down, precision=highest))
    route_probs = jax.nn.softmax(jnp.einsum('sti,ie->ste', normed, router, precision=highest), axis=-1)
    blocks = route_mb.reshape(SEQS, N_DP, LQ)
    expert_ids = jnp.arange(EXPERTS, dtype=jnp.int32)
    picked = (blocks[..., None] == expert_ids).astype(jnp.int32)
    slot_ranks = jnp.cumsum(picked, axis=2) - 1
    slot_pos = lax.optimization_barrier(jnp.sum(slot_ranks * picked, axis=-1))
    kept_mask = slot_pos < CAP
    slot_hot = (slot_pos[..., None] == jnp.arange(CAP, dtype=jnp.int32)) & kept_mask[..., None]
    picked_f = picked.astype(jnp.float32)
    slot_table = picked_f[..., None] * slot_hot.astype(jnp.float32)[..., None, :]
    gate_prob = lax.optimization_barrier(jnp.sum(route_probs.reshape(SEQS, N_DP, LQ, EXPERTS) * picked_f, axis=-1))
    normed_blocks = normed_low.reshape(SEQS, N_DP, LQ, D)
    buffer = low_back(jnp.einsum('sjtec,sjti->jesci', slot_table, normed_blocks, precision=highest))
    expert_upward_projection = low_back(jnp.einsum('jesci,eif->jescf', buffer, expert_input_weights, precision=highest))
    expert_act = low(gelu_tanh(expert_upward_projection))
    expert_res = low(low_back(jnp.einsum('jescf,efi->jesci', expert_act, expert_out, precision=highest)))
    combined = jnp.einsum('sjtec,jesci->sjti', slot_table, expert_res, precision=highest)
    moe_out = (gate_prob[..., None] * combined).reshape(SEQS, LEN, D)
    mix_coef = jax.nn.softmax(jnp.einsum('sti,ik->stk', normed, mix_weight, precision=highest), axis=-1)
    return residual + mix_coef[..., 0:1] * dense_out + mix_coef[..., 1:2] * moe_out

def forward(params, tokens, route_ids):
    w_qkv, w_out, w_up, w_down, router, mix_weight, norm_gains, norm_biases, expert_input_weights, expert_out = params
    results = []
    for index_mb in range(MICRO):
        attend_one = jax.checkpoint(lambda one_seq: attention_apply(one_seq, w_qkv, w_out, norm_gains[:, 0], norm_biases[:, 0]))
        after = lax.map(attend_one, tokens[index_mb])
        results.append(feedforward_block(after, route_ids[index_mb], w_up, w_down, router, mix_weight, norm_gains[:, 1], norm_biases[:, 1], expert_input_weights, expert_out))
    return jnp.stack(results)

def reference(inputs, w_qkv, w_out, w_up, w_down, router, mix_weight, norm_gains, norm_biases, expert_input_weights, expert_out, routes, cotangent):
    params = tuple((arr.astype(jnp.float32) for arr in (w_qkv, w_out, w_up, w_down, router, mix_weight, norm_gains, norm_biases, expert_input_weights, expert_out)))
    tokens = inputs.astype(jnp.float32)
    route_ids = routes[..., 0]
    result, pullback = jax.vjp(lambda par, tok: forward(par, tok, route_ids), params, tokens)
    gradients, d_tokens = pullback(cotangent.astype(jnp.float32))
    return (result.astype(jnp.bfloat16), d_tokens, gradients[0], gradients[1], gradients[2], gradients[3], gradients[4], gradients[5], gradients[6], gradients[7], gradients[8], gradients[9])
```

```python
import functools

import jax
import jax.numpy as jnp
from jax import lax
from jax.experimental import pallas as pl
from jax.experimental.pallas import tpu as pltpu
from jax.sharding import PartitionSpec as P

HEADS = 16
ALL = ("dp", "expert")
epsilon = 1e-05
highest = lax.Precision.HIGHEST
bf16 = jnp.bfloat16
f32 = jnp.float32


def normalize(values, gain_row, bias_row):
    average = jnp.mean(values, axis=-1, keepdims=True)
    centred = values - average
    variance = jnp.mean(centred * centred, axis=-1, keepdims=True)
    inv_std = lax.rsqrt(variance + epsilon)
    scaled = centred * inv_std
    return (scaled * gain_row + bias_row, scaled, inv_std)


def normalize_back(grad_in, scaled, inv_std, gain_row):
    weighted = grad_in * gain_row
    first_mean = jnp.mean(weighted, axis=-1, keepdims=True)
    second = jnp.mean(weighted * scaled, axis=-1, keepdims=True)
    return (
        inv_std * (weighted - first_mean - scaled * second),
        jnp.sum(grad_in * scaled, axis=0),
        jnp.sum(grad_in, axis=0),
    )


def gelu_tanh(values):
    return jax.nn.gelu(values, approximate=True)


def gelu_derivative(values, grad_in):
    unused, pullback = jax.vjp(gelu_tanh, values)
    return pullback(grad_in)[0]


def matmul(left_op, right_op):
    return jnp.dot(left_op, right_op, preferred_element_type=f32)


def inner_rows(left_op, right_op, precision=None):
    return lax.dot_general(
        left_op,
        right_op,
        (((0,), (0,)), ((), ())),
        preferred_element_type=f32,
        precision=precision,
    )


def times_transposed(left_op, right_op, precision=None):
    return lax.dot_general(
        left_op,
        right_op,
        (((1,), (1,)), ((), ())),
        preferred_element_type=f32,
        precision=precision,
    )


def softmax_rows(logits):
    row_max = jnp.max(logits, axis=-1, keepdims=True)
    expo = jnp.exp(logits - row_max)
    return expo / jnp.sum(expo, axis=-1, keepdims=True)


def partner(array, axes, bit):
    count = lax.axis_size(axes)
    return lax.ppermute(array, axes, [(i, i ^ bit) for i in range(count)])


def bits_of(count):
    return [1 << k for k in range(count.bit_length() - 1)]


def dp_gather(block, order):
    have = {0: block}
    for bit in order:
        for rel in list(have):
            have[rel ^ bit] = partner(have[rel], "dp", bit)
    return [have[rel] for rel in range(len(have))]


def dp_scatter(parts, order):
    have = dict(enumerate(parts))
    for step, bit in enumerate(order):
        kept = {}
        for rel in have:
            if rel & bit == 0:
                kept[rel] = have[rel].astype(f32) + partner(
                    have[rel | bit].astype(bf16), "dp", bit
                ).astype(f32)
        have = kept
    return have[0]


def all_scatter(partial, me, order):
    count = lax.axis_size(ALL)
    bits = bits_of(count)[::-1]
    kind = partial.dtype
    block = partial.reshape((2,) * len(bits) + (partial.shape[0] // count,) + partial.shape[1:])
    for step, bit in enumerate(order):
        axis = bits.index(bit)
        bits.remove(bit)
        own_bit = (me // bit) % 2
        kept = lax.dynamic_index_in_dim(block, own_bit, axis, keepdims=False)
        sent = lax.dynamic_index_in_dim(block, 1 - own_bit, axis, keepdims=False)
        got = partner(sent, ALL, bit)
        block = kept.astype(f32) + got.astype(f32)
        if step < len(order) - 1:
            block = block.astype(kind)
    return block


def head_scores(me, q_head, keys, score_scale):
    rows = q_head.shape[0]
    row_at = lax.broadcasted_iota(jnp.int32, (rows, rows), 0) + me * rows
    col_at = lax.broadcasted_iota(jnp.int32, (rows, rows), 1)
    scores = []
    for rel, key in enumerate(keys):
        part = times_transposed(q_head, key) * score_scale
        scores.append(jnp.where(row_at >= col_at + (me ^ rel) * rows, part, -1e30))
    top = functools.reduce(jnp.maximum, [jnp.max(s, axis=-1, keepdims=True) for s in scores])
    expo = [jnp.exp(s - top) for s in scores]
    total = functools.reduce(jnp.add, [jnp.sum(e, axis=-1, keepdims=True) for e in expo])
    return [e / total for e in expo]


def only_head(values, head, head_dim):
    lane = lax.broadcasted_iota(jnp.int32, values.shape, 1)
    return jnp.where(lane // head_dim == head, values, jnp.zeros_like(values))


def attend_kernel(me_ref, q_ref, *refs, blocks, head_dim, score_scale):
    keys, values, out_ref = refs[:blocks], refs[blocks : 2 * blocks], refs[2 * blocks]
    me = me_ref[0]
    pair_width = 2 * head_dim
    for pair in range(q_ref.shape[1] // pair_width):
        lanes = slice(pair * pair_width, (pair + 1) * pair_width)
        q_pair = q_ref[:, lanes]
        k_pair = [k[:, lanes] for k in keys]
        v_pair = [v[:, lanes] for v in values]
        mixed = jnp.zeros(q_pair.shape, f32)
        for head in range(2):
            probs = head_scores(me, only_head(q_pair, head, head_dim), k_pair, score_scale)
            part = functools.reduce(
                jnp.add, [matmul(p.astype(bf16), v) for p, v in zip(probs, v_pair)]
            )
            mixed = mixed + only_head(part, head, head_dim)
        out_ref[:, lanes] = mixed.astype(bf16)


def attend_back_kernel(me_ref, q_ref, do_ref, *refs, blocks, head_dim, score_scale):
    keys, values = refs[:blocks], refs[blocks : 2 * blocks]
    dq_ref = refs[2 * blocks]
    dk_refs = refs[2 * blocks + 1 : 3 * blocks + 1]
    dv_refs = refs[3 * blocks + 1 :]
    me = me_ref[0]
    pair_width = 2 * head_dim
    for pair in range(q_ref.shape[1] // pair_width):
        lanes = slice(pair * pair_width, (pair + 1) * pair_width)
        q_pair = q_ref[:, lanes]
        do_pair = do_ref[:, lanes]
        k_pair = [k[:, lanes] for k in keys]
        v_pair = [v[:, lanes] for v in values]
        d_query = jnp.zeros(q_pair.shape, f32)
        d_keys = [jnp.zeros(q_pair.shape, f32) for _ in range(blocks)]
        d_values = [jnp.zeros(q_pair.shape, f32) for _ in range(blocks)]
        for head in range(2):
            q_head = only_head(q_pair, head, head_dim)
            do_head = only_head(do_pair, head, head_dim)
            probs = head_scores(me, q_head, k_pair, score_scale)
            d_probs = [times_transposed(do_head, v) for v in v_pair]
            delta = functools.reduce(
                jnp.add,
                [jnp.sum(d * p, axis=-1, keepdims=True) for d, p in zip(d_probs, probs)],
            )
            d_part = jnp.zeros(q_pair.shape, f32)
            for rel in range(blocks):
                d_score = (probs[rel] * (d_probs[rel] - delta)).astype(bf16)
                d_part = d_part + matmul(d_score, k_pair[rel])
                d_keys[rel] = d_keys[rel] + inner_rows(d_score, q_head)
                d_values[rel] = d_values[rel] + inner_rows(probs[rel].astype(bf16), do_head)
            d_query = d_query + only_head(d_part, head, head_dim)
        dq_ref[:, lanes] = (d_query * score_scale).astype(bf16)
        for rel in range(blocks):
            dk_refs[rel][:, lanes] = (d_keys[rel] * score_scale).astype(bf16)
            dv_refs[rel][:, lanes] = d_values[rel].astype(bf16)


def attention(me, wide, keys, values, q_rows, extra=None):
    blocks = len(keys)
    tokens, width = keys[0].shape
    head_dim = width // HEADS
    lanes = 4 * head_dim
    spec = pl.BlockSpec((q_rows, lanes), lambda m, h, me_ref: (m, h))
    back = extra is not None
    body = functools.partial(
        attend_back_kernel if back else attend_kernel,
        blocks=blocks,
        head_dim=head_dim,
        score_scale=head_dim ** (-0.5),
    )
    operands = (wide,) + ((extra,) if back else ()) + tuple(keys) + tuple(values)
    one = jax.ShapeDtypeStruct((tokens, width), bf16)
    results = 1 + 2 * blocks if back else 1
    products = 5 if back else 2
    return pl.pallas_call(
        body,
        grid_spec=pltpu.PrefetchScalarGridSpec(
            num_scalar_prefetch=1,
            grid=(tokens // q_rows, width // lanes),
            in_specs=[spec] * len(operands),
            out_specs=[spec] * results,
        ),
        out_shape=[one] * results,
        cost_estimate=pl.CostEstimate(
            flops=products * 4 * tokens * q_rows * blocks * width,
            bytes_accessed=2 * tokens * width * (len(operands) + results),
            transcendentals=tokens * q_rows * blocks * HEADS,
        ),
        name="attend_back" if back else "attend",
    )(me[None], *operands)


def on_device(
    inputs,
    w_qkv,
    w_out,
    w_up,
    w_down,
    router,
    mix_weight,
    norm_gains,
    norm_biases,
    expert_input_weights,
    expert_out,
    routes,
    cotangent,
):
    micro = inputs.shape[0]
    q_rows = inputs.shape[2]
    width = inputs.shape[3]
    n_dp = lax.axis_size("dp")
    n_peers = lax.axis_size("expert")
    local_experts = expert_input_weights.shape[0]
    all_experts = n_peers * local_experts
    capacity = max(2, 3 * q_rows // (2 * all_experts))
    tokens_n = micro * q_rows
    slots = all_experts * capacity
    dp_me = lax.axis_index("dp")
    me = dp_me * n_peers + lax.axis_index("expert")

    dp_bits = bits_of(n_dp)
    all_bits = bits_of(n_dp * n_peers)
    inside, across = all_bits[: len(all_bits) - len(dp_bits)], all_bits[-len(dp_bits) :]
    order_a = inside[:1] + across + inside[1:]
    order_b = inside[:1] + across[::-1] + inside[1:]

    def gather(shard):
        return lax.all_gather(shard, ALL, axis=0, tiled=True)

    small = gather(
        jnp.concatenate(
            [router, mix_weight, norm_gains.astype(bf16), norm_biases.astype(bf16)], axis=1
        )
    )
    full_qkv = gather(w_qkv)
    full_out = gather(w_out)
    full_up = gather(w_up)
    full_down = gather(w_down)
    logits_n = all_experts + 2
    small_f = small.astype(f32)
    heads_f = small_f[:, :logits_n]
    norm_rows = small_f[:, logits_n:].T
    gain1, gain2, bias1, bias2 = [norm_rows[k : k + 1] for k in range(4)]

    tokens = inputs[:, 0].reshape(tokens_n, width).astype(f32)
    normed1, scaled1, inv1 = normalize(tokens, gain1, bias1)
    normed1_b = normed1.astype(bf16)
    key_own = matmul(normed1_b, full_qkv[:, width : 2 * width]).astype(bf16)
    value_own = matmul(normed1_b, full_qkv[:, 2 * width :]).astype(bf16)
    query = matmul(normed1_b, full_qkv[:, :width]).astype(bf16)
    keys = dp_gather(key_own, dp_bits)
    values = dp_gather(value_own, dp_bits[::-1])
    mixed_b = attention(dp_me, query, keys, values, q_rows)[0]
    residual = tokens + matmul(mixed_b, full_out)
    normed2, scaled2, inv2 = normalize(residual, gain2, bias2)
    normed2_b = normed2.astype(bf16)

    route_ids = routes[:, 0, :, 0]
    logits = jnp.dot(normed2, heads_f, precision=highest)
    route_probs = softmax_rows(logits[:, :all_experts])
    mix_coef = softmax_rows(logits[:, all_experts:])
    expert_ids = jnp.arange(all_experts, dtype=jnp.int32)
    slot_ids = jnp.arange(capacity, dtype=jnp.int32)
    picked3 = (route_ids[:, :, None] == expert_ids).astype(f32)
    earlier = jnp.tril(jnp.ones((q_rows, q_rows), f32), -1)
    before = jnp.einsum("ts,mse->mte", earlier, picked3, preferred_element_type=f32)
    slot_pos = jnp.sum(before * picked3, axis=-1).astype(jnp.int32)
    slot_hot = (slot_pos[:, :, None] == slot_ids).astype(f32)
    picked = picked3.reshape(tokens_n, all_experts)
    gate_prob = jnp.sum(route_probs * picked, axis=1, keepdims=True)
    slot_table = (
        (picked3[..., None] * slot_hot[:, :, None, :])
        .reshape(micro, q_rows, slots)
        .astype(bf16)
    )
    d_out = cotangent[:, 0].reshape(tokens_n, width).astype(f32)
    d_moe = d_out * mix_coef[:, 1:2]
    grad_slots = (d_moe * gate_prob).astype(bf16)

    def exchange(rows):
        return lax.all_to_all(rows, "expert", split_axis=0, concat_axis=0, tiled=True)

    def dispatch(rows):
        placed = jnp.einsum(
            "mts,mtd->msd", slot_table, rows.reshape(micro, q_rows, width),
            preferred_element_type=f32,
        ).astype(bf16)
        placed = placed.reshape(micro, n_peers, local_experts * capacity, width)
        return exchange(jnp.swapaxes(placed, 0, 1))

    def at_expert(rows):
        rows = rows.reshape(n_peers, micro, local_experts, capacity, width)
        return rows.transpose(2, 0, 1, 3, 4).reshape(local_experts, -1, width)

    def from_expert(rows):
        rows = rows.reshape(local_experts, n_peers, micro, capacity, width)
        return rows.transpose(1, 2, 0, 3, 4).reshape(
            n_peers, micro, local_experts * capacity, width
        )

    def collect(rows):
        back = jnp.swapaxes(exchange(from_expert(rows)), 0, 1).reshape(micro, slots, width)
        return jnp.einsum(
            "mts,msd->mtd", slot_table, back, preferred_element_type=f32
        ).reshape(tokens_n, width)

    arrived = at_expert(dispatch(normed2_b))
    grad_recv = at_expert(dispatch(grad_slots))

    expert_up = jnp.einsum(
        "xri,xif->xrf", arrived, expert_input_weights, preferred_element_type=f32
    )
    expert_act = gelu_tanh(expert_up).astype(bf16)
    expert_res = jnp.einsum(
        "xrf,xfi->xri", expert_act, expert_out, preferred_element_type=f32
    ).astype(bf16)
    combined = collect(expert_res)
    expert_dact = jnp.einsum(
        "xri,xfi->xrf", grad_recv, expert_out, preferred_element_type=f32
    )
    expert_dup = gelu_derivative(expert_up, expert_dact).astype(bf16)
    expert_din = jnp.einsum(
        "xrf,xif->xri", expert_dup, expert_input_weights, preferred_element_type=f32
    ).astype(bf16)
    from_slots = collect(expert_din)

    up_dense = matmul(normed2_b, full_up)
    act_dense = gelu_tanh(up_dense).astype(bf16)
    dense_out = matmul(act_dense, full_down)
    grad_dense = (d_out * mix_coef[:, 0:1]).astype(bf16)
    d_up = gelu_derivative(up_dense, times_transposed(grad_dense, full_down)).astype(bf16)
    g_down = all_scatter(inner_rows(act_dense, grad_dense).astype(bf16), me, order_a)
    g_up = all_scatter(inner_rows(normed2_b, d_up).astype(bf16), me, order_b)
    d_normed2 = times_transposed(d_up, full_up)

    hidden = expert_act.shape[-1]
    piece = hidden // n_dp

    def piece_of(array, rel):
        return lax.dynamic_slice_in_dim(array, (dp_me ^ rel) * piece, piece, axis=2)

    g_eout = dp_scatter(
        [
            jnp.einsum(
                "xrf,xri->xfi", piece_of(expert_act, rel), grad_recv, preferred_element_type=f32
            )
            for rel in range(n_dp)
        ],
        dp_bits,
    )
    g_ein = dp_scatter(
        [
            jnp.einsum(
                "xri,xrf->xif", arrived, piece_of(expert_dup, rel), preferred_element_type=f32
            )
            for rel in range(n_dp)
        ],
        dp_bits[::-1],
    )

    moe_out = gate_prob * combined
    result = residual + mix_coef[:, 0:1] * dense_out + mix_coef[:, 1:2] * moe_out
    d_coef = jnp.concatenate(
        [
            jnp.sum(d_out * dense_out, axis=1, keepdims=True),
            jnp.sum(d_out * moe_out, axis=1, keepdims=True),
        ],
        axis=1,
    )
    d_mixlog = mix_coef * (d_coef - jnp.sum(mix_coef * d_coef, axis=1, keepdims=True))
    d_gate = jnp.sum(d_moe * combined, axis=1, keepdims=True)
    d_routelog = route_probs * (picked * d_gate - gate_prob * d_gate)
    d_logits = jnp.concatenate([d_routelog, d_mixlog], axis=1)
    g_heads = inner_rows(normed2, d_logits, precision=highest)
    d_normed2 = d_normed2 + from_slots + times_transposed(d_logits, heads_f, precision=highest)
    d_norm2, d_gain2, d_bias2 = normalize_back(d_normed2, scaled2, inv2, gain2)
    d_resid = d_out + d_norm2
    grad_attn = d_resid.astype(bf16)

    d_mixed = times_transposed(grad_attn, full_out).astype(bf16)
    g_out = all_scatter(inner_rows(mixed_b, grad_attn).astype(bf16), me, order_a)
    back = attention(dp_me, query, keys, values, q_rows, extra=d_mixed)
    d_query = back[0]
    d_key = dp_scatter(back[1 : n_dp + 1], dp_bits).astype(bf16)
    d_value = dp_scatter(back[n_dp + 1 :], dp_bits[::-1]).astype(bf16)
    d_qkv = jnp.concatenate([d_query, d_key, d_value], axis=1)
    d_normed1 = times_transposed(d_qkv, full_qkv)
    g_query = all_scatter(inner_rows(normed1_b, d_query).astype(bf16), me, order_a)
    g_key = all_scatter(inner_rows(normed1_b, d_key).astype(bf16), me, order_b)
    g_value = all_scatter(inner_rows(normed1_b, d_value).astype(bf16), me, order_a)
    d_norm1, d_gain1, d_bias1 = normalize_back(d_normed1, scaled1, inv1, gain1)
    d_inputs = d_resid + d_norm1

    g_small = all_scatter(
        jnp.concatenate([g_heads, jnp.stack([d_gain1, d_gain2, d_bias1, d_bias2]).T], axis=1),
        me,
        order_b,
    )
    shape4 = (micro, 1, q_rows, width)
    return (
        result.astype(bf16).reshape(shape4),
        d_inputs.reshape(shape4),
        jnp.concatenate([g_query, g_key, g_value], axis=1),
        g_out,
        g_up,
        g_down,
        g_small[:, :all_experts],
        g_small[:, all_experts:logits_n],
        g_small[:, logits_n : logits_n + 2],
        g_small[:, logits_n + 2 :],
        g_ein,
        g_eout,
    )


def solution(mesh):
    rows = P(ALL, None)
    whole = P(None, "expert", "dp", None)
    return jax.shard_map(
        on_device,
        mesh=mesh,
        in_specs=(whole,)
        + (rows,) * 8
        + (P("expert", None, None), P("expert", None, None), whole, whole),
        out_specs=(whole, whole)
        + (rows,) * 8
        + (P("expert", None, "dp"), P("expert", "dp", None)),
        check_vma=False,
    )
```

```python
import functools

import jax
import jax.numpy as jnp
from jax import lax
from jax.experimental import pallas as pl
from jax.experimental.pallas import tpu as pltpu
from jax.sharding import PartitionSpec as P

HEADS = 16
ALL = ("dp", "expert")
epsilon = 1e-05
highest = lax.Precision.HIGHEST
bf16 = jnp.bfloat16
f32 = jnp.float32


def normalize(values, gain_row, bias_row):
    average = jnp.mean(values, axis=-1, keepdims=True)
    centred = values - average
    variance = jnp.mean(centred * centred, axis=-1, keepdims=True)
    inv_std = lax.rsqrt(variance + epsilon)
    scaled = centred * inv_std
    return (scaled * gain_row + bias_row, scaled, inv_std)


def normalize_back(grad_in, scaled, inv_std, gain_row):
    weighted = grad_in * gain_row
    first_mean = jnp.mean(weighted, axis=-1, keepdims=True)
    second = jnp.mean(weighted * scaled, axis=-1, keepdims=True)
    return (
        inv_std * (weighted - first_mean - scaled * second),
        jnp.sum(grad_in * scaled, axis=0),
        jnp.sum(grad_in, axis=0),
    )


def gelu_tanh(values):
    return jax.nn.gelu(values, approximate=True)


def gelu_derivative(values, grad_in):
    unused, pullback = jax.vjp(gelu_tanh, values)
    return pullback(grad_in)[0]


def matmul(left_op, right_op):
    return jnp.dot(left_op, right_op, preferred_element_type=f32)


def inner_rows(left_op, right_op, precision=None):
    return lax.dot_general(
        left_op,
        right_op,
        (((0,), (0,)), ((), ())),
        preferred_element_type=f32,
        precision=precision,
    )


def times_transposed(left_op, right_op, precision=None):
    return lax.dot_general(
        left_op,
        right_op,
        (((1,), (1,)), ((), ())),
        preferred_element_type=f32,
        precision=precision,
    )


def softmax_rows(logits):
    row_max = jnp.max(logits, axis=-1, keepdims=True)
    expo = jnp.exp(logits - row_max)
    return expo / jnp.sum(expo, axis=-1, keepdims=True)


def partner(array, axes, bit):
    count = lax.axis_size(axes)
    return lax.ppermute(array, axes, [(i, i ^ bit) for i in range(count)])


def bits_of(count):
    return [1 << k for k in range(count.bit_length() - 1)]


def dp_gather(block, order):
    have = {0: block}
    for bit in order:
        for rel in list(have):
            have[rel ^ bit] = partner(have[rel], "dp", bit)
    return [have[rel] for rel in range(len(have))]


def dp_scatter(parts, order):
    have = dict(enumerate(parts))
    for step, bit in enumerate(order):
        kept = {}
        for rel in have:
            if rel & bit == 0:
                kept[rel] = have[rel].astype(f32) + partner(
                    have[rel | bit].astype(bf16), "dp", bit
                ).astype(f32)
        have = kept
    return have[0]


def all_assemble(shard, me, order):
    count = lax.axis_size(ALL)
    bits = bits_of(count)[::-1]
    block = shard.reshape((1,) * len(bits) + shard.shape)
    for bit in order:
        axis = bits.index(bit)
        got = partner(block, ALL, bit)
        block = jnp.where(
            (me // bit) % 2 == 0,
            jnp.concatenate([block, got], axis=axis),
            jnp.concatenate([got, block], axis=axis),
        )
    return block.reshape((count * shard.shape[0],) + shard.shape[1:])


def all_scatter(partial, me, order):
    count = lax.axis_size(ALL)
    bits = bits_of(count)[::-1]
    kind = partial.dtype
    block = partial.reshape((2,) * len(bits) + (partial.shape[0] // count,) + partial.shape[1:])
    for step, bit in enumerate(order):
        axis = bits.index(bit)
        bits.remove(bit)
        own_bit = (me // bit) % 2
        kept = lax.dynamic_index_in_dim(block, own_bit, axis, keepdims=False)
        sent = lax.dynamic_index_in_dim(block, 1 - own_bit, axis, keepdims=False)
        got = partner(sent, ALL, bit)
        block = kept.astype(f32) + got.astype(f32)
        if step < len(order) - 1:
            block = block.astype(kind)
    return block


def head_scores(me, q_head, keys, score_scale):
    rows = q_head.shape[0]
    row_at = lax.broadcasted_iota(jnp.int32, (rows, rows), 0) + me * rows
    col_at = lax.broadcasted_iota(jnp.int32, (rows, rows), 1)
    scores = []
    for rel, key in enumerate(keys):
        part = times_transposed(q_head, key) * score_scale
        scores.append(jnp.where(row_at >= col_at + (me ^ rel) * rows, part, -1e30))
    top = functools.reduce(jnp.maximum, [jnp.max(s, axis=-1, keepdims=True) for s in scores])
    expo = [jnp.exp(s - top) for s in scores]
    total = functools.reduce(jnp.add, [jnp.sum(e, axis=-1, keepdims=True) for e in expo])
    return [e / total for e in expo]


def only_head(values, head, head_dim):
    lane = lax.broadcasted_iota(jnp.int32, values.shape, 1)
    return jnp.where(lane // head_dim == head, values, jnp.zeros_like(values))


def key_pair(kv_refs, pair, pair_width, group):
    at = pair * pair_width
    keys = [kv[0, :, at : at + pair_width] for kv in kv_refs]
    values = [kv[0, :, group + at : group + at + pair_width] for kv in kv_refs]
    return keys, values


def attend_kernel(me_ref, q_ref, *refs, blocks, head_dim, score_scale):
    kv_refs, out_ref = refs[:blocks], refs[blocks]
    me = me_ref[0]
    pair_width = 2 * head_dim
    group = q_ref.shape[1]
    for pair in range(group // pair_width):
        lanes = slice(pair * pair_width, (pair + 1) * pair_width)
        q_pair = q_ref[:, lanes]
        k_pair, v_pair = key_pair(kv_refs, pair, pair_width, group)
        mixed = jnp.zeros(q_pair.shape, f32)
        for head in range(2):
            probs = head_scores(me, only_head(q_pair, head, head_dim), k_pair, score_scale)
            part = functools.reduce(
                jnp.add, [matmul(p.astype(bf16), v) for p, v in zip(probs, v_pair)]
            )
            mixed = mixed + only_head(part, head, head_dim)
        out_ref[:, lanes] = mixed.astype(bf16)


def attend_back_kernel(me_ref, q_ref, do_ref, *refs, blocks, head_dim, score_scale):
    kv_refs, dq_ref, dkv_ref = refs[:blocks], refs[blocks], refs[blocks + 1]
    me = me_ref[0]
    pair_width = 2 * head_dim
    group = q_ref.shape[1]
    for pair in range(group // pair_width):
        lanes = slice(pair * pair_width, (pair + 1) * pair_width)
        v_lanes = slice(group + pair * pair_width, group + (pair + 1) * pair_width)
        q_pair = q_ref[:, lanes]
        do_pair = do_ref[:, lanes]
        k_pair, v_pair = key_pair(kv_refs, pair, pair_width, group)
        d_query = jnp.zeros(q_pair.shape, f32)
        d_keys = [jnp.zeros(q_pair.shape, f32) for _ in range(blocks)]
        d_values = [jnp.zeros(q_pair.shape, f32) for _ in range(blocks)]
        for head in range(2):
            q_head = only_head(q_pair, head, head_dim)
            do_head = only_head(do_pair, head, head_dim)
            probs = head_scores(me, q_head, k_pair, score_scale)
            d_probs = [times_transposed(do_head, v) for v in v_pair]
            delta = functools.reduce(
                jnp.add,
                [jnp.sum(d * p, axis=-1, keepdims=True) for d, p in zip(d_probs, probs)],
            )
            d_part = jnp.zeros(q_pair.shape, f32)
            for rel in range(blocks):
                d_score = (probs[rel] * (d_probs[rel] - delta)).astype(bf16)
                d_part = d_part + matmul(d_score, k_pair[rel])
                d_keys[rel] = d_keys[rel] + inner_rows(d_score, q_head)
                d_values[rel] = d_values[rel] + inner_rows(probs[rel].astype(bf16), do_head)
            d_query = d_query + only_head(d_part, head, head_dim)
        dq_ref[:, lanes] = (d_query * score_scale).astype(bf16)
        for rel in range(blocks):
            dkv_ref[rel, :, lanes] = (d_keys[rel] * score_scale).astype(bf16)
            dkv_ref[rel, :, v_lanes] = d_values[rel].astype(bf16)


def attention(me, query, kv_all, group, q_rows, extra=None):
    blocks = kv_all.shape[0]
    tokens, width = query.shape
    head_dim = width // HEADS
    rows_spec = pl.BlockSpec((q_rows, group), lambda m, h, me_ref: (m, h))

    def kv_spec(rel):
        return pl.BlockSpec((1, q_rows, 2 * group), lambda m, h, me_ref: (rel, m, h))

    back = extra is not None
    body = functools.partial(
        attend_back_kernel if back else attend_kernel,
        blocks=blocks,
        head_dim=head_dim,
        score_scale=head_dim ** (-0.5),
    )
    rows_in = (query,) + ((extra,) if back else ())
    out_specs = [rows_spec]
    out_shape = [jax.ShapeDtypeStruct((tokens, width), bf16)]
    if back:
        out_specs.append(pl.BlockSpec((blocks, q_rows, 2 * group), lambda m, h, me_ref: (0, m, h)))
        out_shape.append(jax.ShapeDtypeStruct(kv_all.shape, bf16))
    products = 5 if back else 2
    return pl.pallas_call(
        body,
        grid_spec=pltpu.PrefetchScalarGridSpec(
            num_scalar_prefetch=1,
            grid=(tokens // q_rows, width // group),
            in_specs=[rows_spec] * len(rows_in) + [kv_spec(rel) for rel in range(blocks)],
            out_specs=out_specs,
        ),
        out_shape=out_shape,
        cost_estimate=pl.CostEstimate(
            flops=products * 4 * tokens * q_rows * blocks * width,
            bytes_accessed=2 * tokens * width * (2 + 4 * blocks),
            transcendentals=tokens * q_rows * blocks * HEADS,
        ),
        name="attend_back" if back else "attend",
    )(me[None], *rows_in, *([kv_all] * blocks))


def on_device(
    inputs,
    w_qkv,
    w_out,
    w_up,
    w_down,
    router,
    mix_weight,
    norm_gains,
    norm_biases,
    expert_input_weights,
    expert_out,
    routes,
    cotangent,
):
    micro = inputs.shape[0]
    q_rows = inputs.shape[2]
    width = inputs.shape[3]
    n_dp = lax.axis_size("dp")
    n_peers = lax.axis_size("expert")
    local_experts = expert_input_weights.shape[0]
    all_experts = n_peers * local_experts
    capacity = max(2, 3 * q_rows // (2 * all_experts))
    tokens_n = micro * q_rows
    slots = all_experts * capacity
    group = 4 * (width // HEADS)
    groups_n = width // group
    dp_me = lax.axis_index("dp")
    me = dp_me * n_peers + lax.axis_index("expert")

    dp_bits = bits_of(n_dp)
    all_bits = bits_of(n_dp * n_peers)
    inside, across = all_bits[: len(all_bits) - len(dp_bits)], all_bits[-len(dp_bits) :]
    order_a = inside[:1] + across + inside[1:]
    order_b = inside[:1] + across[::-1] + inside[1:]

    def gather(shard):
        return lax.all_gather(shard, ALL, axis=0, tiled=True)

    def grouped(shard):
        rows = shard.shape[0]
        parts = shard.reshape(rows, 3, groups_n, group)
        kv = jnp.stack([parts[:, 1], parts[:, 2]], axis=2).reshape(rows, 2 * width)
        return jnp.concatenate([shard[:, :width], kv], axis=1)

    def ungrouped(rows_qkv):
        rows = rows_qkv.shape[0]
        kv = rows_qkv[:, width:].reshape(rows, groups_n, 2, group)
        return jnp.concatenate(
            [
                rows_qkv[:, :width],
                kv[:, :, 0].reshape(rows, width),
                kv[:, :, 1].reshape(rows, width),
            ],
            axis=1,
        )

    small = all_assemble(
        jnp.concatenate(
            [router, mix_weight, norm_gains.astype(bf16), norm_biases.astype(bf16)], axis=1
        ),
        me,
        order_a[::-1],
    )
    full_qkv = gather(grouped(w_qkv))
    full_out = gather(w_out)
    full_up = gather(w_up)
    full_down = gather(w_down)
    full_q, full_kv = full_qkv[:, :width], full_qkv[:, width:]
    logits_n = all_experts + 2
    small_f = small.astype(f32)
    heads_f = small_f[:, :logits_n]
    norm_rows = small_f[:, logits_n:].T
    gain1, gain2, bias1, bias2 = [norm_rows[k : k + 1] for k in range(4)]

    inputs_own = inputs[:, 0].reshape(tokens_n, width)
    inputs_all = jnp.concatenate(dp_gather(inputs_own, dp_bits), axis=0)
    tokens = inputs_own.astype(f32)
    normed1, scaled1, inv1 = normalize(tokens, gain1, bias1)
    normed1_b = normed1.astype(bf16)
    normed1_all = normalize(inputs_all.astype(f32), gain1, bias1)[0].astype(bf16)
    query = matmul(normed1_b, full_q).astype(bf16)
    kv_all = matmul(normed1_all, full_kv).astype(bf16).reshape(n_dp, tokens_n, 2 * width)
    mixed_b = attention(dp_me, query, kv_all, group, q_rows)[0]
    residual = tokens + matmul(mixed_b, full_out)
    normed2, scaled2, inv2 = normalize(residual, gain2, bias2)
    normed2_b = normed2.astype(bf16)

    route_ids = routes[:, 0, :, 0]
    logits = jnp.dot(normed2, heads_f, precision=highest)
    route_probs = softmax_rows(logits[:, :all_experts])
    mix_coef = softmax_rows(logits[:, all_experts:])
    expert_ids = jnp.arange(all_experts, dtype=jnp.int32)
    slot_ids = jnp.arange(capacity, dtype=jnp.int32)
    picked3 = (route_ids[:, :, None] == expert_ids).astype(f32)
    earlier = jnp.tril(jnp.ones((q_rows, q_rows), f32), -1)
    before = jnp.einsum("ts,mse->mte", earlier, picked3, preferred_element_type=f32)
    slot_pos = jnp.sum(before * picked3, axis=-1).astype(jnp.int32)
    slot_hot = (slot_pos[:, :, None] == slot_ids).astype(f32)
    picked = picked3.reshape(tokens_n, all_experts)
    gate_prob = jnp.sum(route_probs * picked, axis=1, keepdims=True)
    slot_table = (
        (picked3[..., None] * slot_hot[:, :, None, :])
        .reshape(micro, q_rows, slots)
        .astype(bf16)
    )
    d_out = cotangent[:, 0].reshape(tokens_n, width).astype(f32)
    d_moe = d_out * mix_coef[:, 1:2]
    grad_slots = (d_moe * gate_prob).astype(bf16)

    def exchange(rows):
        return lax.all_to_all(rows, "expert", split_axis=0, concat_axis=0, tiled=True)

    def placed(rows):
        return jnp.einsum(
            "mts,mtd->msd", slot_table, rows.reshape(micro, q_rows, width),
            preferred_element_type=f32,
        ).astype(bf16).reshape(micro, n_peers, local_experts * capacity, width)

    def at_expert(rows):
        rows = rows.reshape(n_peers, micro, local_experts, capacity, width)
        return rows.transpose(2, 0, 1, 3, 4).reshape(local_experts, -1, width)

    def from_expert(rows):
        rows = rows.reshape(local_experts, n_peers, micro, capacity, width)
        return rows.transpose(1, 2, 0, 3, 4).reshape(
            n_peers, micro, local_experts * capacity, width
        )

    def collected(rows):
        back = jnp.swapaxes(rows, 0, 1).reshape(micro, slots, width)
        return jnp.einsum(
            "mts,msd->mtd", slot_table, back, preferred_element_type=f32
        ).reshape(tokens_n, width)

    sent = jnp.concatenate([placed(normed2_b), placed(grad_slots)], axis=0)
    got = exchange(jnp.swapaxes(sent, 0, 1))
    arrived = at_expert(got[:, :micro])
    grad_recv = at_expert(got[:, micro:])

    def expert_forward(rows, weights):
        return jnp.einsum("xri,xif->xrf", rows, weights, preferred_element_type=f32)

    def expert_backward(up, grads, weights):
        d_act = jnp.einsum("xri,xfi->xrf", grads, weights, preferred_element_type=f32)
        return gelu_derivative(up, d_act).astype(bf16)

    expert_up = expert_forward(arrived, expert_input_weights)
    expert_act = gelu_tanh(expert_up).astype(bf16)
    expert_res = jnp.einsum(
        "xrf,xfi->xri", expert_act, expert_out, preferred_element_type=f32
    ).astype(bf16)
    expert_dup = expert_backward(expert_up, grad_recv, expert_out)
    expert_din = jnp.einsum(
        "xrf,xif->xri", expert_dup, expert_input_weights, preferred_element_type=f32
    ).astype(bf16)
    returned = exchange(
        jnp.concatenate([from_expert(expert_res), from_expert(expert_din)], axis=1)
    )
    combined = collected(returned[:, :micro])
    from_slots = collected(returned[:, micro:])

    up_dense = matmul(normed2_b, full_up)
    act_dense = gelu_tanh(up_dense).astype(bf16)
    dense_out = matmul(act_dense, full_down)
    grad_dense = (d_out * mix_coef[:, 0:1]).astype(bf16)
    d_up = gelu_derivative(up_dense, times_transposed(grad_dense, full_down)).astype(bf16)
    g_down = all_scatter(inner_rows(act_dense, grad_dense).astype(bf16), me, order_a)
    g_up = all_scatter(inner_rows(normed2_b, d_up).astype(bf16), me, order_b)
    d_normed2 = times_transposed(d_up, full_up)

    piece = expert_out.shape[1] // n_dp
    arrived_all = jnp.concatenate(dp_gather(arrived, dp_bits), axis=1)
    grad_all = jnp.concatenate(dp_gather(grad_recv, dp_bits[::-1]), axis=1)
    in_piece = lax.dynamic_slice_in_dim(expert_input_weights, dp_me * piece, piece, axis=2)
    out_piece = lax.dynamic_slice_in_dim(expert_out, dp_me * piece, piece, axis=1)
    up_piece = expert_forward(arrived_all, in_piece)
    act_piece = gelu_tanh(up_piece).astype(bf16)
    dup_piece = expert_backward(up_piece, grad_all, out_piece)
    g_eout = jnp.einsum("xrf,xri->xfi", act_piece, grad_all, preferred_element_type=f32)
    g_ein = jnp.einsum("xri,xrf->xif", arrived_all, dup_piece, preferred_element_type=f32)

    moe_out = gate_prob * combined
    result = residual + mix_coef[:, 0:1] * dense_out + mix_coef[:, 1:2] * moe_out
    d_coef = jnp.concatenate(
        [
            jnp.sum(d_out * dense_out, axis=1, keepdims=True),
            jnp.sum(d_out * moe_out, axis=1, keepdims=True),
        ],
        axis=1,
    )
    d_mixlog = mix_coef * (d_coef - jnp.sum(mix_coef * d_coef, axis=1, keepdims=True))
    d_gate = jnp.sum(d_moe * combined, axis=1, keepdims=True)
    d_routelog = route_probs * (picked * d_gate - gate_prob * d_gate)
    d_logits = jnp.concatenate([d_routelog, d_mixlog], axis=1)
    g_heads = inner_rows(normed2, d_logits, precision=highest)
    d_normed2 = d_normed2 + from_slots + times_transposed(d_logits, heads_f, precision=highest)
    d_norm2, d_gain2, d_bias2 = normalize_back(d_normed2, scaled2, inv2, gain2)
    d_resid = d_out + d_norm2
    grad_attn = d_resid.astype(bf16)

    d_mixed = times_transposed(grad_attn, full_out).astype(bf16)
    g_out = all_scatter(inner_rows(mixed_b, grad_attn).astype(bf16), me, order_b)
    d_query, d_kv = attention(dp_me, query, kv_all, group, q_rows, extra=d_mixed)
    d_kv = d_kv.reshape(n_dp * tokens_n, 2 * width)
    g_query = all_scatter(inner_rows(normed1_b, d_query).astype(bf16), me, order_a)
    g_kv = [
        all_scatter(inner_rows(normed1_all, d_kv[:, part]).astype(bf16), me, order)
        for part, order in ((slice(0, width), order_b), (slice(width, 2 * width), order_a))
    ]
    d_normed1_all = times_transposed(d_kv, full_kv).reshape(n_dp, tokens_n, width)
    d_normed1_parts = [d_normed1_all[rel] for rel in range(n_dp)]
    d_normed1 = dp_scatter(d_normed1_parts, dp_bits) + times_transposed(d_query, full_q)
    d_norm1, d_gain1, d_bias1 = normalize_back(d_normed1, scaled1, inv1, gain1)
    d_inputs = d_resid + d_norm1

    g_small = all_scatter(
        jnp.concatenate([g_heads, jnp.stack([d_gain1, d_gain2, d_bias1, d_bias2]).T], axis=1),
        me,
        order_b,
    )
    shape4 = (micro, 1, q_rows, width)
    return (
        result.astype(bf16).reshape(shape4),
        d_inputs.reshape(shape4),
        ungrouped(jnp.concatenate([g_query] + g_kv, axis=1)),
        g_out,
        g_up,
        g_down,
        g_small[:, :all_experts],
        g_small[:, all_experts:logits_n],
        g_small[:, logits_n : logits_n + 2],
        g_small[:, logits_n + 2 :],
        g_ein,
        g_eout,
    )


def solution(mesh):
    rows = P(ALL, None)
    whole = P(None, "expert", "dp", None)
    return jax.shard_map(
        on_device,
        mesh=mesh,
        in_specs=(whole,)
        + (rows,) * 8
        + (P("expert", None, None), P("expert", None, None), whole, whole),
        out_specs=(whole, whole)
        + (rows,) * 8
        + (P("expert", None, "dp"), P("expert", "dp", None)),
        check_vma=False,
    )
```
